32 devices in a mesh: occ: 16 (over z, y, x), grp: 2 (over core).
Axes of the slice: x: 2, y: 2, z: 4, core: 2. Of those that a mesh axis runs over, the one named last changes fastest.
Arguments:
- b_factors: bfloat16 [32, 512, 768], P(('occ', 'grp')), may hold values from -0.29882812 to 0.29882812
- occ_energy: float32 [32], replicated, may hold values from -2 to -0.5
- vir_energy: float32 [512], replicated, may hold values from 0.2 to 3
- integrals: bfloat16 [512, 768, 1024], P('grp', 'occ'), may hold values from -0.0625 to 0.0625
- window_start: int32 [1], replicated, may hold values from 0 to 15
Outputs:
- aux_metric: float32 [768, 768], P('occ', 'grp')
- lagrangian: float32 [32, 1024], P('occ', 'grp')
The draws below stay inside these ranges and needn't reach their ends.
Inputs may be any that keep to these rules, and one draw needn't show every extreme that they name: `window_start`: the cycle offset of the window's first pair.
All inputs are finite; a program needn't handle non-finite values.
Results may differ from the reference program's by a relative error of at most 0.0034.
Values may be sent and summed in bfloat16 or wider, within the bound.
A program may use at most 128 MiB of HBM per device.

```python
import math
import jax
import jax.numpy as jnp
from jax import lax

V = 512
NAUX = 768
NORB = 1024
SHIFTS = 3
O = 32
N_OCC = 16
N_GRP = 2


def steps_of(stream_key, dims, pieces, smallest, top_value):
    def one(position, shards_of):
        steps = jax.random.uniform(jax.random.fold_in(jax.random.fold_in(stream_key, 6), position), (shards_of,), jnp.float32, smallest / len(pieces), top_value / len(pieces))
        return jnp.repeat(jnp.exp(steps), dims[position] // shards_of).reshape((-1,) + (1,) * (len(dims) - position - 1))

    gain = one(*pieces[0])
    for cut in pieces[1:]:
        gain = gain * one(*cut)
    return gain


def noise(rng, shape, spread, reach, cuts=(), held_as=jnp.bfloat16):
    values = spread * jax.random.normal(rng, shape, jnp.float32)
    if cuts:
        values = values * steps_of(rng, shape, cuts, -0.22, 0.18)
    return jnp.clip(values, -reach, reach).astype(held_as)


def setup_inputs(seed: int = 0) -> dict:
    arg_keys = jax.random.split(jax.random.key(seed), 6)
    b_factors = noise(arg_keys[0], (O, V, NAUX), 0.05, 0.29882812, ((0, 32),))
    occ_energy = jnp.clip(jax.random.uniform(arg_keys[1], (O,), jnp.float32, -2.0, -0.5), -2.0, -0.5)
    vir_energy = jnp.clip(jnp.exp(jax.random.uniform(arg_keys[2], (V,), jnp.float32, math.log(0.2), math.log(3.0))), 0.2, 3.0)
    integrals = noise(arg_keys[3], (V, NAUX, NORB), (V * NAUX // 50) ** -0.5, 0.0625, ((0, 2), (1, 16)))
    window_start = jax.random.randint(arg_keys[4], (1,), 0, N_OCC).astype(jnp.int32)
    return {"b_factors": b_factors, "occ_energy": occ_energy, "vir_energy": vir_energy, "integrals": integrals, "window_start": window_start}


def reference(b_factors, occ_energy, vir_energy, integrals, window_start):
    offset = window_start[0]

    def per_orbital(orbital):
        cycle_pos = orbital // N_GRP
        group_pos = orbital % N_GRP
        own_rows = b_factors[orbital]
        total = jnp.zeros((V, NAUX), jnp.float32)
        for step_no in range(SHIFTS):
            partner = (jnp.mod(cycle_pos - offset - step_no, N_OCC) * N_GRP + group_pos).astype(jnp.int32)
            other_rows = lax.dynamic_index_in_dim(b_factors, partner, 0, keepdims=False)
            intersection = lax.dot_general(own_rows, other_rows, (((1,), (1,)), ((), ())), preferred_element_type=jnp.float32)
            denominator = occ_energy[orbital] + occ_energy[partner] - vir_energy[:, None] - vir_energy[None, :]
            amplitude = intersection / denominator
            combined = (2.0 * amplitude - amplitude.T).astype(jnp.bfloat16)
            total = total + jnp.dot(combined, other_rows, preferred_element_type=jnp.float32)
        return total.astype(jnp.bfloat16)

    density = lax.map(per_orbital, jnp.arange(O, dtype=jnp.int32))
    flat_density = density.reshape(O * V, NAUX)
    aux_metric = jnp.dot(flat_density.T, b_factors.reshape(O * V, NAUX), preferred_element_type=jnp.float32)
    lagrangian = jnp.dot(density.reshape(O, V * NAUX), integrals.reshape(V * NAUX, NORB), preferred_element_type=jnp.float32)
    return aux_metric, lagrangian
```

```python
import functools

import jax
import jax.numpy as jnp
from jax import lax
from jax.experimental import pallas as pl
from jax.experimental.pallas import tpu as pltpu
from jax.sharding import PartitionSpec as P

SHIFTS = 3
MESH = pl.DeviceIdType.MESH


def shifted(x, axis, by):
    size = lax.axis_size(axis)
    return lax.ppermute(x, axis, [(i, (i + by) % size) for i in range(size)])


def exchange_kernel(
    n_cycle, n_group, step_cols,
    dens_ref, aux_ref, int_ref, aux_out, lag_out,
    dens_recv, dens_f32, pair_recv, aux_send, aux_recv, int_vmem, lag_acc, lag_send, lag_recv,
    int_sem, dens_ss, dens_rs, pair_ss, pair_rs, aux_ss, aux_rs, lag_ss, lag_rs,
):
    cyc = lax.axis_index("occ")
    grp = lax.axis_index("grp")
    n_dev = n_cycle * n_group
    me = cyc * n_group + grp
    rows = dens_recv.shape[1]
    depth = step_cols * 128
    n_steps = rows // step_cols

    def int_copy(k):
        part = pl.ds(pl.multiple_of(k * depth, depth), depth)
        return pltpu.make_async_copy(int_ref.at[part], int_vmem.at[part], int_sem.at[k])

    @pl.loop(0, n_steps)
    def _(k):
        int_copy(k).start()

    barrier = pltpu.get_barrier_semaphore()

    @pl.loop(1, n_dev)
    def _(s):
        d = lax.rem(me + s, n_dev)
        pl.semaphore_signal(
            barrier, inc=1, device_id=(d // n_group, lax.rem(d, n_group)), device_id_type=MESH
        )

    pl.semaphore_wait(barrier, n_dev - 1)

    def pair_copy(s):
        g = lax.rem(grp + s, n_group)
        return pltpu.make_async_remote_copy(
            src_ref=aux_ref.at[g], dst_ref=pair_recv.at[s - 1],
            send_sem=pair_ss.at[s - 1], recv_sem=pair_rs.at[s - 1],
            device_id=(cyc, g), device_id_type=MESH,
        )

    def dens_copy(s):
        d = lax.rem(me + s, n_dev)
        o, g = d // n_group, lax.rem(d, n_group)
        return pltpu.make_async_remote_copy(
            src_ref=dens_ref.at[d], dst_ref=dens_recv.at[s - 1],
            send_sem=dens_ss.at[s - 1], recv_sem=dens_rs.at[s - 1],
            device_id=(o, g), device_id_type=MESH,
        )

    def aux_copy(s):
        o = lax.rem(cyc + s, n_cycle)
        return pltpu.make_async_remote_copy(
            src_ref=aux_send.at[o], dst_ref=aux_recv.at[s - 1],
            send_sem=aux_ss.at[s - 1], recv_sem=aux_rs.at[s - 1],
            device_id=(o, grp), device_id_type=MESH,
        )

    def lag_copy(s):
        d = lax.rem(me + s, n_dev)
        o, g = d // n_group, lax.rem(d, n_group)
        return pltpu.make_async_remote_copy(
            src_ref=lag_send.at[d], dst_ref=lag_recv.at[s - 1],
            send_sem=lag_ss.at[s - 1], recv_sem=lag_rs.at[s - 1],
            device_id=(o, g), device_id_type=MESH,
        )

    @pl.loop(1, n_group)
    def _(s):
        pair_copy(s).start()

    @pl.loop(1, n_dev)
    def _(s):
        dens_copy(s).start()

    @pl.loop(1, n_group)
    def _(s):
        pair_copy(s).wait_recv()

    @pl.loop(0, n_cycle)
    def _(o):
        block = aux_ref[grp, o]
        for s in range(n_group - 1):
            block = block + pair_recv[s, o]
        aux_send[o] = block.astype(aux_send.dtype)

    aux_total = aux_ref[grp, cyc]
    for s in range(n_group - 1):
        aux_total = aux_total + pair_recv[s, cyc]
    aux_out[...] = aux_total

    @pl.loop(1, n_cycle)
    def _(s):
        aux_copy(s).start()

    own_at = pl.ds(pl.multiple_of(me * rows, rows), rows)
    dens_f32[own_at, :] = dens_ref[me].astype(jnp.float32)

    @pl.loop(1, n_dev)
    def _(s):
        dens_copy(s).wait_recv()
        source = lax.rem(me - s + n_dev, n_dev)
        at = pl.ds(pl.multiple_of(source * rows, rows), rows)
        dens_f32[at, :] = dens_recv[s - 1].astype(jnp.float32)

    lag_acc[...] = jnp.zeros_like(lag_acc)

    @pl.loop(0, n_steps)
    def _(k):
        int_copy(k).wait()
        pieces = [
            dens_f32[pl.ds(k * step_cols + j, n_dev, stride=rows), :] for j in range(step_cols)
        ]
        left = jnp.concatenate(pieces, axis=1).astype(jnp.bfloat16)
        part = pl.ds(pl.multiple_of(k * depth, depth), depth)
        lag_acc[...] += jnp.dot(left, int_vmem[part, :], preferred_element_type=jnp.float32)

    orb_block = lag_out.shape[1]
    for o in range(n_cycle):
        for g in range(n_group):
            lag_send[o * n_group + g] = lag_acc[
                o * n_group:(o + 1) * n_group, g * orb_block:(g + 1) * orb_block
            ]

    @pl.loop(1, n_dev)
    def _(s):
        lag_copy(s).start()

    @pl.loop(1, n_cycle)
    def _(s):
        aux_copy(s).wait_recv()
        aux_out[...] += aux_recv[s - 1].astype(jnp.float32)

    lag_out[...] = lag_send[me]

    @pl.loop(1, n_dev)
    def _(s):
        lag_copy(s).wait_recv()
        lag_out[...] += lag_recv[s - 1]

    @pl.loop(1, n_group)
    def _(s):
        pair_copy(s).wait_send()

    @pl.loop(1, n_cycle)
    def _(s):
        aux_copy(s).wait_send()

    @pl.loop(1, n_dev)
    def _(s):
        dens_copy(s).wait_send()
        lag_copy(s).wait_send()


def exchange(n_cycle, n_group, dens_blocks, aux_parts, int_rows):
    n_dev, rows, _ = dens_blocks.shape
    _, _, row_block, col_block = aux_parts.shape
    depth, n_orb = int_rows.shape
    orb_block = n_orb // n_group
    step_cols = next(c for c in (6, 4, 3, 2, 1) if rows % c == 0)
    vmem = pl.BlockSpec(memory_space=pltpu.VMEM)
    dma = pltpu.SemaphoreType.DMA
    return pl.pallas_call(
        functools.partial(exchange_kernel, n_cycle, n_group, step_cols),
        out_shape=(
            jax.ShapeDtypeStruct((row_block, col_block), jnp.float32),
            jax.ShapeDtypeStruct((n_group, orb_block), jnp.float32),
        ),
        in_specs=[vmem, vmem, pl.BlockSpec(memory_space=pl.ANY)],
        out_specs=(vmem, vmem),
        scratch_shapes=[
            pltpu.VMEM((n_dev - 1, rows, 128), jnp.bfloat16),
            pltpu.VMEM((n_dev * rows, 128), jnp.float32),
            pltpu.VMEM((n_group - 1, n_cycle, row_block, col_block), jnp.float32),
            pltpu.VMEM((n_cycle, row_block, col_block), jnp.bfloat16),
            pltpu.VMEM((n_cycle - 1, row_block, col_block), jnp.bfloat16),
            pltpu.VMEM((depth, n_orb), jnp.bfloat16),
            pltpu.VMEM((n_dev, n_orb), jnp.float32),
            pltpu.VMEM((n_dev, n_group, orb_block), jnp.float32),
            pltpu.VMEM((n_dev - 1, n_group, orb_block), jnp.float32),
            dma((rows // step_cols,)),
            dma((n_dev - 1,)), dma((n_dev - 1,)),
            dma((n_group - 1,)), dma((n_group - 1,)),
            dma((n_cycle - 1,)), dma((n_cycle - 1,)),
            dma((n_dev - 1,)), dma((n_dev - 1,)),
        ],
        compiler_params=pltpu.CompilerParams(
            collective_id=0, has_side_effects=True, vmem_limit_bytes=58 * 1024 * 1024
        ),
    )(dens_blocks, aux_parts, int_rows)


def local(b_factors, occ_energy, vir_energy, integrals, window_start):
    n_cycle = lax.axis_size("occ")
    n_group = lax.axis_size("grp")
    cycle_pos = lax.axis_index("occ")
    group_pos = lax.axis_index("grp")
    offset = jnp.mod(window_start[0], n_cycle)
    every_orbital = jnp.arange(occ_energy.shape[0], dtype=jnp.int32)
    own_index = cycle_pos * n_group + group_pos
    own_energy = jnp.sum(jnp.where(every_orbital == own_index, occ_energy, 0.0))
    own_rows = b_factors[0]
    rotated = lax.switch(
        offset,
        [(lambda x: x)]
        + [functools.partial(lambda by, x: shifted(x, "occ", by), by) for by in range(1, n_cycle)],
        own_rows,
    )
    total = jnp.zeros(own_rows.shape, jnp.float32)
    for step_no in range(SHIFTS):
        other_rows = shifted(rotated, "occ", step_no) if step_no > 0 else rotated
        partner = jnp.mod(cycle_pos - offset - step_no, n_cycle) * n_group + group_pos
        other_energy = jnp.sum(jnp.where(every_orbital == partner, occ_energy, 0.0))
        intersection = lax.dot_general(
            own_rows, other_rows, (((1,), (1,)), ((), ())), preferred_element_type=jnp.float32
        )
        denominator = own_energy + other_energy - vir_energy[:, None] - vir_energy[None, :]
        amplitude = intersection / denominator
        combined = (2.0 * amplitude - amplitude.T).astype(jnp.bfloat16)
        total = total + jnp.dot(combined, other_rows, preferred_element_type=jnp.float32)
    density = total.astype(jnp.bfloat16)
    aux_term = lax.dot_general(
        density, own_rows, (((0,), (0,)), ((), ())), preferred_element_type=jnp.float32
    )
    n_vir, n_aux = density.shape
    n_dev = n_cycle * n_group
    aux_local = n_aux // n_cycle
    dens_blocks = (
        density.reshape(n_vir, n_cycle, aux_local)
        .transpose(1, 0, 2)
        .reshape(n_dev, n_vir // n_group * aux_local // 128, 128)
    )
    aux_parts = aux_term.reshape(
        n_cycle, n_aux // n_cycle, n_group, n_aux // n_group
    ).transpose(2, 0, 1, 3)
    int_rows = integrals.reshape(-1, integrals.shape[2])
    return exchange(n_cycle, n_group, dens_blocks, aux_parts, int_rows)


def solution(mesh):
    placed = (P(("occ", "grp"), None, None), P(), P(), P("grp", "occ", None), P())
    return jax.shard_map(
        local,
        mesh=mesh,
        in_specs=placed,
        out_specs=(P("occ", "grp"), P("occ", "grp")),
        check_vma=False,
    )
```

```python
import functools

import jax
import jax.numpy as jnp
from jax import lax
from jax.experimental import pallas as pl
from jax.experimental.pallas import tpu as pltpu
from jax.sharding import PartitionSpec as P

SHIFTS = 3
MESH = pl.DeviceIdType.MESH


def shifted(x, axis, by):
    size = lax.axis_size(axis)
    return lax.ppermute(x, axis, [(i, (i + by) % size) for i in range(size)])


def pair_kernel(
    n_cycle, chunks,
    own_ref, rot_ref, energy_ref, vir_col_ref, vir_row_ref, dens_out,
    near, far, total, near_ss, near_rs, far_ss, far_rs,
):
    cyc = lax.axis_index("occ")
    grp = lax.axis_index("grp")
    odd = lax.rem(cyc, 2)
    mate = cyc + 1 - 2 * odd
    ahead = lax.rem(cyc + 2, n_cycle)
    behind = lax.rem(cyc + n_cycle - 2, n_cycle)
    size = own_ref.shape[0] // chunks
    barrier = pltpu.get_barrier_semaphore()
    for other in (mate, ahead, behind):
        pl.semaphore_signal(barrier, inc=1, device_id=(other, grp), device_id_type=MESH)
    pl.semaphore_wait(barrier, 3)

    def part(c):
        return pl.ds(c * size, size)

    def far_copy(c):
        return pltpu.make_async_remote_copy(
            src_ref=rot_ref.at[part(c)], dst_ref=far.at[part(c)],
            send_sem=far_ss.at[c], recv_sem=far_rs.at[c],
            device_id=(ahead, grp), device_id_type=MESH,
        )

    def near_copy(c, source):
        return pltpu.make_async_remote_copy(
            src_ref=source.at[part(c)], dst_ref=near.at[part(c)],
            send_sem=near_ss.at[c], recv_sem=near_rs.at[c],
            device_id=(mate, grp), device_id_type=MESH,
        )

    for c in range(chunks):
        far_copy(c).start()

        @pl.when(odd == 0)
        def _():
            near_copy(c, rot_ref).start()

    n_vir = own_ref.shape[0]
    tall = min(256, n_vir)
    across = (((1,), (1,)), ((), ()))

    def term(other, step_no, put):
        @pl.loop(0, n_vir // tall)
        def _(k):
            at = pl.ds(pl.multiple_of(k * tall, tall), tall)
            straight = lax.dot_general(
                own_ref[at, :], other[...], across, preferred_element_type=jnp.float32
            )
            crossed = lax.dot_general(
                other[at, :], own_ref[...], across, preferred_element_type=jnp.float32
            )
            denominator = energy_ref[step_no] - vir_col_ref[at, :] - vir_row_ref[...]
            combined = ((2.0 * straight - crossed) / denominator).astype(jnp.bfloat16)
            put(at, jnp.dot(combined, other[...], preferred_element_type=jnp.float32))

    def put_first(at, value):
        total[at, :] = value

    def put_next(at, value):
        total[at, :] += value

    def put_last(at, value):
        dens_out[at, :] = (total[at, :] + value).astype(dens_out.dtype)

    term(rot_ref, 0, put_first)
    for c in range(chunks):
        far_copy(c).wait_recv()

        @pl.when(odd == 1)
        def _():
            near_copy(c, far).start()

    term(far, 2, put_next)
    for c in range(chunks):
        near_copy(c, rot_ref).wait_recv()
    term(near, 1, put_last)
    for c in range(chunks):
        far_copy(c).wait_send()
        near_copy(c, rot_ref).wait_send()


def pair_densities(n_cycle, own_rows, rotated, energies, vir_energy):
    n_vir, n_aux = own_rows.shape
    chunks = 4
    vmem = pl.BlockSpec(memory_space=pltpu.VMEM)
    dma = pltpu.SemaphoreType.DMA
    block = pltpu.VMEM((n_vir, n_aux), jnp.bfloat16)
    return pl.pallas_call(
        functools.partial(pair_kernel, n_cycle, chunks),
        out_shape=jax.ShapeDtypeStruct((n_vir, n_aux), jnp.bfloat16),
        in_specs=[vmem, vmem, pl.BlockSpec(memory_space=pltpu.SMEM), vmem, vmem],
        out_specs=vmem,
        scratch_shapes=[
            block, block, pltpu.VMEM((n_vir, n_aux), jnp.float32),
            dma((chunks,)), dma((chunks,)), dma((chunks,)), dma((chunks,)),
        ],
        compiler_params=pltpu.CompilerParams(
            collective_id=0, has_side_effects=True, vmem_limit_bytes=40 * 1024 * 1024
        ),
    )(own_rows, rotated, energies, vir_energy[:, None], vir_energy[None, :])


def exchange_kernel(
    n_cycle, n_group, inner, halves, step_cols,
    blocks_ref, dens_ref, own_ref, int_ref, aux_out, lag_out,
    dens_recv, dens_f32, pair_send, pair_recv, aux_sum, plane_send, plane_recv, plane_sum,
    line_send, line_recv, int_vmem, lag_acc, lag_send, lag_recv,
    int_sem, dens_ss, dens_rs, pair_ss, pair_rs, plane_ss, plane_rs, line_ss, line_rs,
    lag_ss, lag_rs,
):
    cyc = lax.axis_index("occ")
    grp = lax.axis_index("grp")
    n_dev = n_cycle * n_group
    me = cyc * n_group + grp
    outer = n_cycle // inner
    seat = lax.rem(cyc, inner)
    plane = cyc // inner
    rows = blocks_ref.shape[1]
    half_rows = rows // halves
    depth = step_cols * 128
    n_steps = rows // step_cols

    def int_copy(k):
        part = pl.ds(pl.multiple_of(k * depth, depth), depth)
        return pltpu.make_async_copy(int_ref.at[part], int_vmem.at[part], int_sem.at[k])

    barrier = pltpu.get_barrier_semaphore()

    @pl.loop(1, n_dev)
    def _(s):
        d = lax.rem(me + s, n_dev)
        pl.semaphore_signal(
            barrier, inc=1, device_id=(d // n_group, lax.rem(d, n_group)), device_id_type=MESH
        )

    @pl.loop(0, n_steps)
    def _(k):
        int_copy(k).start()

    pl.semaphore_wait(barrier, n_dev - 1)

    def dens_copy(h, s):
        d = lax.rem(me + s, n_dev)
        part = pl.ds(h * half_rows, half_rows)
        return pltpu.make_async_remote_copy(
            src_ref=blocks_ref.at[d, part], dst_ref=dens_recv.at[s - 1, part],
            send_sem=dens_ss.at[h, s - 1], recv_sem=dens_rs.at[h, s - 1],
            device_id=(d // n_group, lax.rem(d, n_group)), device_id_type=MESH,
        )

    def pair_copy(s):
        return pltpu.make_async_remote_copy(
            src_ref=pair_send.at[s - 1], dst_ref=pair_recv.at[s - 1],
            send_sem=pair_ss.at[s - 1], recv_sem=pair_rs.at[s - 1],
            device_id=(cyc, lax.rem(grp + s, n_group)), device_id_type=MESH,
        )

    def plane_copy(s):
        q = lax.rem(seat + s, inner)
        return pltpu.make_async_remote_copy(
            src_ref=plane_send.at[s - 1], dst_ref=plane_recv.at[s - 1],
            send_sem=plane_ss.at[s - 1], recv_sem=plane_rs.at[s - 1],
            device_id=(plane * inner + q, grp), device_id_type=MESH,
        )

    def line_copy(s):
        z = lax.rem(plane + s, outer)
        return pltpu.make_async_remote_copy(
            src_ref=line_send.at[s - 1], dst_ref=line_recv.at[s - 1],
            send_sem=line_ss.at[s - 1], recv_sem=line_rs.at[s - 1],
            device_id=(z * inner + seat, grp), device_id_type=MESH,
        )

    def lag_copy(s):
        d = lax.rem(me + s, n_dev)
        return pltpu.make_async_remote_copy(
            src_ref=lag_send.at[d], dst_ref=lag_recv.at[s - 1],
            send_sem=lag_ss.at[s - 1], recv_sem=lag_rs.at[s - 1],
            device_id=(d // n_group, lax.rem(d, n_group)), device_id_type=MESH,
        )

    for h in range(halves):
        @pl.loop(1, n_dev)
        def _(s):
            dens_copy(h, s).start()

    def aux_columns(g):
        return lax.dot_general(
            dens_ref[...], own_ref[g], (((0,), (0,)), ((), ())),
            preferred_element_type=jnp.float32,
        ).reshape(aux_sum.shape)

    for s in range(1, n_group):
        pair_send[s - 1] = aux_columns(lax.rem(grp + s, n_group))
        pair_copy(s).start()
    aux_sum[...] = aux_columns(grp)
    for s in range(1, n_group):
        pair_copy(s).wait_recv()

        @pl.loop(0, n_cycle)
        def _(o):
            aux_sum[o] += pair_recv[s - 1, o]

    for s in range(1, inner):
        q = lax.rem(seat + s, inner)

        @pl.loop(0, outer)
        def _(z):
            plane_send[s - 1, z] = aux_sum[z * inner + q].astype(plane_send.dtype)

        plane_copy(s).start()

    def take_half(h):
        part = pl.ds(h * half_rows, half_rows)
        own_at = pl.ds(me * rows + h * half_rows, half_rows)
        dens_f32[own_at, :] = blocks_ref[me, part].astype(jnp.float32)

        @pl.loop(1, n_dev)
        def _(s):
            dens_copy(h, s).wait_recv()
            source = lax.rem(me - s + n_dev, n_dev)
            at = pl.ds(source * rows + h * half_rows, half_rows)
            dens_f32[at, :] = dens_recv[s - 1, part].astype(jnp.float32)

        steps = n_steps // halves

        @pl.loop(h * steps, (h + 1) * steps)
        def _(k):
            int_copy(k).wait()
            pieces = [
                dens_f32[pl.ds(k * step_cols + j, n_dev, stride=rows), :]
                for j in range(step_cols)
            ]
            left = jnp.concatenate(pieces, axis=1).astype(jnp.bfloat16)
            at = pl.ds(pl.multiple_of(k * depth, depth), depth)
            lag_acc[...] += jnp.dot(left, int_vmem[at, :], preferred_element_type=jnp.float32)

    lag_acc[...] = jnp.zeros_like(lag_acc)
    for h in range(halves - 1):
        take_half(h)

    for s in range(1, inner):
        plane_copy(s).wait_recv()

    @pl.loop(0, outer)
    def _(z):
        block = aux_sum[z * inner + seat]
        for s in range(1, inner):
            block = block + plane_recv[s - 1, z].astype(jnp.float32)
        plane_sum[z] = block

    for s in range(1, outer):
        line_send[s - 1] = plane_sum[lax.rem(plane + s, outer)].astype(line_send.dtype)
        line_copy(s).start()

    take_half(halves - 1)

    orb_block = lag_out.shape[1]
    for o in range(n_cycle):
        for g in range(n_group):
            lag_send[o * n_group + g] = lag_acc[
                o * n_group:(o + 1) * n_group, g * orb_block:(g + 1) * orb_block
            ]

    @pl.loop(1, n_dev)
    def _(s):
        lag_copy(s).start()

    aux_total = plane_sum[plane]
    for s in range(1, outer):
        line_copy(s).wait_recv()
        aux_total = aux_total + line_recv[s - 1].astype(jnp.float32)
    aux_out[...] = aux_total

    lag_out[...] = lag_send[me]

    @pl.loop(1, n_dev)
    def _(s):
        lag_copy(s).wait_recv()
        lag_out[...] += lag_recv[s - 1]

    for s in range(1, n_group):
        pair_copy(s).wait_send()
    for s in range(1, inner):
        plane_copy(s).wait_send()
    for s in range(1, outer):
        line_copy(s).wait_send()

    @pl.loop(1, n_dev)
    def _(s):
        for h in range(halves):
            dens_copy(h, s).wait_send()
        lag_copy(s).wait_send()


def exchange(n_cycle, n_group, dens_blocks, density, own_columns, int_rows):
    n_dev, rows, _ = dens_blocks.shape
    n_vir, n_aux = density.shape
    row_block = n_aux // n_cycle
    col_block = n_aux // n_group
    depth, n_orb = int_rows.shape
    orb_block = n_orb // n_group
    halves = 2 if rows % 32 == 0 else 1
    step_cols = next(c for c in (6, 4, 3, 2, 1) if (rows // halves) % c == 0)
    inner = 4 if n_cycle % 4 == 0 else 1
    outer = n_cycle // inner
    tile = (row_block, col_block)
    vmem = pl.BlockSpec(memory_space=pltpu.VMEM)
    dma = pltpu.SemaphoreType.DMA
    return pl.pallas_call(
        functools.partial(exchange_kernel, n_cycle, n_group, inner, halves, step_cols),
        out_shape=(
            jax.ShapeDtypeStruct(tile, jnp.float32),
            jax.ShapeDtypeStruct((n_group, orb_block), jnp.float32),
        ),
        in_specs=[vmem, vmem, vmem, pl.BlockSpec(memory_space=pl.ANY)],
        out_specs=(vmem, vmem),
        scratch_shapes=[
            pltpu.VMEM((n_dev - 1, rows, 128), jnp.bfloat16),
            pltpu.VMEM((n_dev * rows, 128), jnp.float32),
            pltpu.VMEM((n_group - 1, n_cycle) + tile, jnp.float32),
            pltpu.VMEM((n_group - 1, n_cycle) + tile, jnp.float32),
            pltpu.VMEM((n_cycle,) + tile, jnp.float32),
            pltpu.VMEM((inner - 1, outer) + tile, jnp.bfloat16),
            pltpu.VMEM((inner - 1, outer) + tile, jnp.bfloat16),
            pltpu.VMEM((outer,) + tile, jnp.float32),
            pltpu.VMEM((outer - 1,) + tile, jnp.bfloat16),
            pltpu.VMEM((outer - 1,) + tile, jnp.bfloat16),
            pltpu.VMEM((depth, n_orb), jnp.bfloat16),
            pltpu.VMEM((n_dev, n_orb), jnp.float32),
            pltpu.VMEM((n_dev, n_group, orb_block), jnp.float32),
            pltpu.VMEM((n_dev - 1, n_group, orb_block), jnp.float32),
            dma((rows // step_cols,)),
            dma((halves, n_dev - 1)), dma((halves, n_dev - 1)),
            dma((n_group - 1,)), dma((n_group - 1,)),
            dma((inner - 1,)), dma((inner - 1,)),
            dma((outer - 1,)), dma((outer - 1,)),
            dma((n_dev - 1,)), dma((n_dev - 1,)),
        ],
        compiler_params=pltpu.CompilerParams(
            collective_id=1, has_side_effects=True, vmem_limit_bytes=58 * 1024 * 1024
        ),
    )(dens_blocks, density, own_columns, int_rows)


def local(b_factors, occ_energy, vir_energy, integrals, window_start):
    n_cycle = lax.axis_size("occ")
    n_group = lax.axis_size("grp")
    cycle_pos = lax.axis_index("occ")
    group_pos = lax.axis_index("grp")
    offset = jnp.mod(window_start[0], n_cycle)
    every_orbital = jnp.arange(occ_energy.shape[0], dtype=jnp.int32)
    own_index = cycle_pos * n_group + group_pos
    own_rows = b_factors[0]
    n_vir, n_aux = own_rows.shape
    rotated = lax.switch(
        offset,
        [(lambda x: x)]
        + [functools.partial(lambda by, x: shifted(x, "occ", by), by) for by in range(1, n_cycle)],
        own_rows,
    )
    partners = (
        jnp.mod(cycle_pos - offset - jnp.arange(SHIFTS, dtype=jnp.int32), n_cycle) * n_group
        + group_pos
    )
    own_energy = jnp.sum(jnp.where(every_orbital == own_index, occ_energy, 0.0))
    energies = own_energy + jnp.sum(
        jnp.where(every_orbital[None, :] == partners[:, None], occ_energy[None, :], 0.0), axis=1
    )
    density = pair_densities(n_cycle, own_rows, rotated, energies, vir_energy)
    aux_local = n_aux // n_cycle
    dens_blocks = (
        density.reshape(n_vir, n_cycle, aux_local)
        .transpose(1, 0, 2)
        .reshape(n_cycle * n_group, n_vir // n_group * aux_local // 128, 128)
    )
    own_columns = own_rows.reshape(n_vir, n_group, n_aux // n_group).transpose(1, 0, 2)
    int_rows = integrals.reshape(-1, integrals.shape[2])
    return exchange(n_cycle, n_group, dens_blocks, density, own_columns, int_rows)


def solution(mesh):
    placed = (P(("occ", "grp"), None, None), P(), P(), P("grp", "occ", None), P())
    return jax.shard_map(
        local,
        mesh=mesh,
        in_specs=placed,
        out_specs=(P("occ", "grp"), P("occ", "grp")),
        check_vma=False,
    )
```

```python
import functools
import math

import jax
import jax.numpy as jnp
from jax import lax
from jax.experimental import pallas as pl
from jax.experimental.pallas import tpu as pltpu
from jax.sharding import PartitionSpec as P

MESH = pl.DeviceIdType.MESH


def shifted(x, axis, by):
    size = lax.axis_size(axis)
    return lax.ppermute(x, axis, [(i, (i + by) % size) for i in range(size)])


def block_plan(n_vir, n_aux, n_cycle, n_group):
    aux_local, vir_local = n_aux // n_cycle, n_vir // n_group
    joined = 128 // math.gcd(aux_local, 128)
    lanes = joined * aux_local // 128
    halves = 2 if vir_local % (32 * joined) == 0 else 1
    return aux_local, vir_local, joined, lanes, halves, vir_local // joined // halves


def pair_kernel(
    n_cycle, n_group, chunks,
    own_ref, rot_ref, energy_ref, start_ref, vir_row_ref, dens_out, blocks_out,
    near, far, total, stage, vir_col_ref, near_ss, near_rs, far_ss, far_rs,
):
    cyc = lax.axis_index("occ")
    grp = lax.axis_index("grp")
    odd = lax.rem(cyc, 2)
    mate = cyc + 1 - 2 * odd
    ahead = lax.rem(cyc + 2, n_cycle)
    behind = lax.rem(cyc + n_cycle - 2, n_cycle)
    size = own_ref.shape[0] // chunks
    barrier = pltpu.get_barrier_semaphore()
    for other in (mate, ahead, behind):
        pl.semaphore_signal(barrier, inc=1, device_id=(other, grp), device_id_type=MESH)
    pl.semaphore_wait(barrier, 3)

    def part(c):
        return pl.ds(c * size, size)

    def far_copy(c):
        return pltpu.make_async_remote_copy(
            src_ref=rot_ref.at[part(c)], dst_ref=far.at[part(c)],
            send_sem=far_ss.at[c], recv_sem=far_rs.at[c],
            device_id=(ahead, grp), device_id_type=MESH,
        )

    def near_copy(c, source):
        return pltpu.make_async_remote_copy(
            src_ref=source.at[part(c)], dst_ref=near.at[part(c)],
            send_sem=near_ss.at[c], recv_sem=near_rs.at[c],
            device_id=(mate, grp), device_id_type=MESH,
        )

    for c in range(chunks):
        far_copy(c).start()

        @pl.when(odd == 0)
        def _():
            near_copy(c, rot_ref).start()

    n_vir, n_aux = own_ref.shape
    vir_col_ref[...] = jnp.broadcast_to(vir_row_ref[...], (128, n_vir)).T
    shift = lax.rem(start_ref[0], n_cycle)
    own_energy = energy_ref[cyc * n_group + grp]
    tall = min(256, n_vir)
    across = (((1,), (1,)), ((), ()))

    def term(other, step_no, put):
        place = lax.rem(cyc - shift - step_no + 2 * n_cycle, n_cycle)
        energy = own_energy + energy_ref[place * n_group + grp]

        @pl.loop(0, n_vir // tall)
        def _(k):
            at = pl.ds(pl.multiple_of(k * tall, tall), tall)
            straight = lax.dot_general(
                own_ref[at, :], other[...], across, preferred_element_type=jnp.float32
            )
            crossed = lax.dot_general(
                other[at, :], own_ref[...], across, preferred_element_type=jnp.float32
            )
            denominator = energy - vir_col_ref[at, 0:1] - vir_row_ref[...]
            combined = ((2.0 * straight - crossed) / denominator).astype(jnp.bfloat16)
            put(at, jnp.dot(combined, other[...], preferred_element_type=jnp.float32))

    def put_first(at, value):
        total[at, :] = value

    def put_next(at, value):
        total[at, :] += value

    def put_last(at, value):
        value = total[at, :] + value
        for b in range(n_aux // 128):
            stage[pl.ds(b * n_vir + at.start, tall), :] = value[:, b * 128:(b + 1) * 128]
        dens_out[at, :] = value.astype(dens_out.dtype)

    term(rot_ref, 0, put_first)
    for c in range(chunks):
        far_copy(c).wait_recv()

        @pl.when(odd == 1)
        def _():
            near_copy(c, far).start()

    term(far, 2, put_next)
    for c in range(chunks):
        near_copy(c, rot_ref).wait_recv()
    term(near, 1, put_last)

    aux_local, vir_local, joined, lanes, halves, tall_block = block_plan(
        n_vir, n_aux, n_cycle, n_group
    )

    @pl.loop(0, n_group * halves)
    def _(k):
        g, h = k // halves, lax.rem(k, halves)
        first = k * (tall_block * joined)
        picked = [
            jnp.concatenate(
                [
                    stage[pl.ds(b * n_vir + first + j, tall_block, stride=joined), :]
                    for b in range(n_aux // 128)
                ],
                axis=1,
            )
            for j in range(joined)
        ]
        for o in range(n_cycle):
            wide = jnp.concatenate(
                [piece[:, o * aux_local:(o + 1) * aux_local] for piece in picked], axis=1
            ).astype(blocks_out.dtype)
            for c in range(lanes):
                blocks_out[o * n_group + g, h * lanes + c] = wide[:, c * 128:(c + 1) * 128]

    for c in range(chunks):
        far_copy(c).wait_send()
        near_copy(c, rot_ref).wait_send()


def pair_densities(n_cycle, n_group, own_rows, rotated, occ_energy, vir_energy, window_start):
    n_vir, n_aux = own_rows.shape
    chunks = 4
    _, _, _, lanes, halves, tall_block = block_plan(n_vir, n_aux, n_cycle, n_group)
    smem = pl.BlockSpec(memory_space=pltpu.SMEM)
    vmem = pl.BlockSpec(memory_space=pltpu.VMEM)
    dma = pltpu.SemaphoreType.DMA
    block = pltpu.VMEM((n_vir, n_aux), jnp.bfloat16)
    return pl.pallas_call(
        functools.partial(pair_kernel, n_cycle, n_group, chunks),
        out_shape=(
            jax.ShapeDtypeStruct((n_vir, n_aux), jnp.bfloat16),
            jax.ShapeDtypeStruct(
                (n_cycle * n_group, halves * lanes, tall_block, 128), jnp.bfloat16
            ),
        ),
        in_specs=[vmem, vmem, smem, smem, vmem],
        out_specs=(vmem, vmem),
        scratch_shapes=[
            block, block, pltpu.VMEM((n_vir, n_aux), jnp.float32),
            pltpu.VMEM((n_aux // 128 * n_vir, 128), jnp.float32),
            pltpu.VMEM((n_vir, 128), jnp.float32),
            dma((chunks,)), dma((chunks,)), dma((chunks,)), dma((chunks,)),
        ],
        compiler_params=pltpu.CompilerParams(
            collective_id=0, has_side_effects=True, vmem_limit_bytes=40 * 1024 * 1024
        ),
    )(own_rows, rotated, occ_energy, window_start, vir_energy[None, :])


def exchange_kernel(
    n_cycle, n_group, inner, halves, lanes, step_rows,
    blocks_ref, dens_ref, own_ref, int_ref, aux_out, lag_out,
    dens_recv, dens_f32, pair_send, pair_recv, aux_sum, plane_send, plane_recv, plane_sum,
    line_send, line_recv, int_vmem, lag_acc, lag_send, lag_recv,
    int_sem, dens_ss, dens_rs, pair_ss, pair_rs, plane_ss, plane_rs, line_ss, line_rs,
    lag_ss, lag_rs,
):
    cyc = lax.axis_index("occ")
    grp = lax.axis_index("grp")
    n_dev = n_cycle * n_group
    me = cyc * n_group + grp
    outer = n_cycle // inner
    seat = lax.rem(cyc, inner)
    plane = cyc // inner
    tall_block = blocks_ref.shape[2]
    half_rows = lanes * tall_block
    rows = halves * half_rows
    depth = step_rows * lanes * 128
    n_steps = halves * tall_block // step_rows

    def int_copy(k):
        part = pl.ds(pl.multiple_of(k * depth, depth), depth)
        return pltpu.make_async_copy(int_ref.at[part], int_vmem.at[part], int_sem.at[k])

    barrier = pltpu.get_barrier_semaphore()

    @pl.loop(1, n_dev)
    def _(s):
        d = lax.rem(me + s, n_dev)
        pl.semaphore_signal(
            barrier, inc=1, device_id=(d // n_group, lax.rem(d, n_group)), device_id_type=MESH
        )

    @pl.loop(0, n_steps)
    def _(k):
        int_copy(k).start()

    pl.semaphore_wait(barrier, n_dev - 1)

    def dens_copy(h, s):
        d = lax.rem(me + s, n_dev)
        part = pl.ds(h * lanes, lanes)
        return pltpu.make_async_remote_copy(
            src_ref=blocks_ref.at[d, part], dst_ref=dens_recv.at[s - 1, part],
            send_sem=dens_ss.at[h, s - 1], recv_sem=dens_rs.at[h, s - 1],
            device_id=(d // n_group, lax.rem(d, n_group)), device_id_type=MESH,
        )

    def pair_copy(s):
        return pltpu.make_async_remote_copy(
            src_ref=pair_send.at[s - 1], dst_ref=pair_recv.at[s - 1],
            send_sem=pair_ss.at[s - 1], recv_sem=pair_rs.at[s - 1],
            device_id=(cyc, lax.rem(grp + s, n_group)), device_id_type=MESH,
        )

    def plane_copy(s):
        q = lax.rem(seat + s, inner)
        return pltpu.make_async_remote_copy(
            src_ref=plane_send.at[s - 1], dst_ref=plane_recv.at[s - 1],
            send_sem=plane_ss.at[s - 1], recv_sem=plane_rs.at[s - 1],
            device_id=(plane * inner + q, grp), device_id_type=MESH,
        )

    def line_copy(s):
        z = lax.rem(plane + s, outer)
        return pltpu.make_async_remote_copy(
            src_ref=line_send.at[s - 1], dst_ref=line_recv.at[s - 1],
            send_sem=line_ss.at[s - 1], recv_sem=line_rs.at[s - 1],
            device_id=(z * inner + seat, grp), device_id_type=MESH,
        )

    def lag_copy(s):
        d = lax.rem(me + s, n_dev)
        return pltpu.make_async_remote_copy(
            src_ref=lag_send.at[d], dst_ref=lag_recv.at[s - 1],
            send_sem=lag_ss.at[s - 1], recv_sem=lag_rs.at[s - 1],
            device_id=(d // n_group, lax.rem(d, n_group)), device_id_type=MESH,
        )

    for h in range(halves):
        @pl.loop(1, n_dev)
        def _(s):
            dens_copy(h, s).start()

    def own_part(g):
        width = aux_out.shape[1]
        if len(own_ref.shape) == 3:
            return own_ref[g]
        return own_ref[:, pl.ds(pl.multiple_of(g * width, 128), width)]

    def aux_columns(g):
        return lax.dot_general(
            dens_ref[...], own_part(g), (((0,), (0,)), ((), ())),
            preferred_element_type=jnp.float32,
        ).reshape(aux_sum.shape)

    for s in range(1, n_group):
        pair_send[s - 1] = aux_columns(lax.rem(grp + s, n_group))
        pair_copy(s).start()
    aux_sum[...] = aux_columns(grp)
    for s in range(1, n_group):
        pair_copy(s).wait_recv()

        @pl.loop(0, n_cycle)
        def _(o):
            aux_sum[o] += pair_recv[s - 1, o]

    for s in range(1, inner):
        q = lax.rem(seat + s, inner)

        @pl.loop(0, outer)
        def _(z):
            plane_send[s - 1, z] = aux_sum[z * inner + q].astype(plane_send.dtype)

        plane_copy(s).start()

    def take_half(h):
        part = pl.ds(h * lanes, lanes)
        own_at = pl.ds(me * rows + h * half_rows, half_rows)
        own_block = blocks_ref[me, part].astype(jnp.float32)
        dens_f32[own_at, :] = own_block.reshape(half_rows, 128)

        @pl.loop(1, n_dev)
        def _(s):
            dens_copy(h, s).wait_recv()
            source = lax.rem(me - s + n_dev, n_dev)
            at = pl.ds(source * rows + h * half_rows, half_rows)
            block = dens_recv[s - 1, part].astype(jnp.float32)
            dens_f32[at, :] = block.reshape(half_rows, 128)

        steps = n_steps // halves

        @pl.loop(h * steps, (h + 1) * steps)
        def _(k):
            int_copy(k).wait()
            pieces = [
                dens_f32[
                    pl.ds(
                        h * half_rows + c * tall_block + (k - h * steps) * step_rows + j,
                        n_dev, stride=rows,
                    ), :
                ]
                for j in range(step_rows) for c in range(lanes)
            ]
            left = jnp.concatenate(pieces, axis=1).astype(jnp.bfloat16)
            at = pl.ds(pl.multiple_of(k * depth, depth), depth)
            lag_acc[...] += jnp.dot(left, int_vmem[at, :], preferred_element_type=jnp.float32)

    lag_acc[...] = jnp.zeros_like(lag_acc)
    for h in range(halves - 1):
        take_half(h)

    for s in range(1, inner):
        plane_copy(s).wait_recv()

    @pl.loop(0, outer)
    def _(z):
        block = aux_sum[z * inner + seat]
        for s in range(1, inner):
            block = block + plane_recv[s - 1, z].astype(jnp.float32)
        plane_sum[z] = block

    for s in range(1, outer):
        line_send[s - 1] = plane_sum[lax.rem(plane + s, outer)].astype(line_send.dtype)
        line_copy(s).start()

    take_half(halves - 1)

    orb_block = lag_out.shape[1]
    for o in range(n_cycle):
        for g in range(n_group):
            lag_send[o * n_group + g] = lag_acc[
                o * n_group:(o + 1) * n_group, g * orb_block:(g + 1) * orb_block
            ]

    @pl.loop(1, n_dev)
    def _(s):
        lag_copy(s).start()

    aux_total = plane_sum[plane]
    for s in range(1, outer):
        line_copy(s).wait_recv()
        aux_total = aux_total + line_recv[s - 1].astype(jnp.float32)
    aux_out[...] = aux_total

    lag_out[...] = lag_send[me]

    @pl.loop(1, n_dev)
    def _(s):
        lag_copy(s).wait_recv()
        lag_out[...] += lag_recv[s - 1]

    for s in range(1, n_group):
        pair_copy(s).wait_send()
    for s in range(1, inner):
        plane_copy(s).wait_send()
    for s in range(1, outer):
        line_copy(s).wait_send()

    @pl.loop(1, n_dev)
    def _(s):
        for h in range(halves):
            dens_copy(h, s).wait_send()
        lag_copy(s).wait_send()


def exchange(n_cycle, n_group, dens_blocks, density, own_columns, int_rows):
    n_dev = dens_blocks.shape[0]
    n_vir, n_aux = density.shape
    row_block = n_aux // n_cycle
    col_block = n_aux // n_group
    depth, n_orb = int_rows.shape
    orb_block = n_orb // n_group
    _, _, _, lanes, halves, tall_block = block_plan(n_vir, n_aux, n_cycle, n_group)
    step_rows = 2 if tall_block % 2 == 0 else 1
    rows = halves * lanes * tall_block
    inner = 4 if n_cycle % 4 == 0 else 1
    outer = n_cycle // inner
    tile = (row_block, col_block)
    vmem = pl.BlockSpec(memory_space=pltpu.VMEM)
    dma = pltpu.SemaphoreType.DMA
    return pl.pallas_call(
        functools.partial(
            exchange_kernel, n_cycle, n_group, inner, halves, lanes, step_rows
        ),
        out_shape=(
            jax.ShapeDtypeStruct(tile, jnp.float32),
            jax.ShapeDtypeStruct((n_group, orb_block), jnp.float32),
        ),
        in_specs=[vmem, vmem, vmem, pl.BlockSpec(memory_space=pl.ANY)],
        out_specs=(vmem, vmem),
        scratch_shapes=[
            pltpu.VMEM((n_dev - 1,) + dens_blocks.shape[1:], jnp.bfloat16),
            pltpu.VMEM((n_dev * rows, 128), jnp.float32),
            pltpu.VMEM((n_group - 1, n_cycle) + tile, jnp.float32),
            pltpu.VMEM((n_group - 1, n_cycle) + tile, jnp.float32),
            pltpu.VMEM((n_cycle,) + tile, jnp.float32),
            pltpu.VMEM((inner - 1, outer) + tile, jnp.bfloat16),
            pltpu.VMEM((inner - 1, outer) + tile, jnp.bfloat16),
            pltpu.VMEM((outer,) + tile, jnp.float32),
            pltpu.VMEM((outer - 1,) + tile, jnp.bfloat16),
            pltpu.VMEM((outer - 1,) + tile, jnp.bfloat16),
            pltpu.VMEM((depth, n_orb), jnp.bfloat16),
            pltpu.VMEM((n_dev, n_orb), jnp.float32),
            pltpu.VMEM((n_dev, n_group, orb_block), jnp.float32),
            pltpu.VMEM((n_dev - 1, n_group, orb_block), jnp.float32),
            dma((halves * tall_block // step_rows,)),
            dma((halves, n_dev - 1)), dma((halves, n_dev - 1)),
            dma((n_group - 1,)), dma((n_group - 1,)),
            dma((inner - 1,)), dma((inner - 1,)),
            dma((outer - 1,)), dma((outer - 1,)),
            dma((n_dev - 1,)), dma((n_dev - 1,)),
        ],
        compiler_params=pltpu.CompilerParams(
            collective_id=1, has_side_effects=True, vmem_limit_bytes=58 * 1024 * 1024
        ),
    )(dens_blocks, density, own_columns, int_rows)


def local(b_factors, occ_energy, vir_energy, integrals, window_start):
    n_cycle = lax.axis_size("occ")
    n_group = lax.axis_size("grp")
    offset = jnp.mod(window_start[0], n_cycle)
    own_rows = b_factors[0]
    n_vir, n_aux = own_rows.shape
    rotated = lax.switch(
        offset,
        [(lambda x: x)]
        + [functools.partial(lambda by, x: shifted(x, "occ", by), by) for by in range(1, n_cycle)],
        own_rows,
    )
    density, dens_blocks = pair_densities(
        n_cycle, n_group, own_rows, rotated, occ_energy, vir_energy, window_start
    )
    col_block = n_aux // n_group
    own_columns = own_rows
    if col_block % 128:
        own_columns = own_rows.reshape(n_vir, n_group, col_block).transpose(1, 0, 2)
    int_rows = integrals.reshape(-1, integrals.shape[2])
    return exchange(n_cycle, n_group, dens_blocks, density, own_columns, int_rows)


def solution(mesh):
    placed = (P(("occ", "grp"), None, None), P(), P(), P("grp", "occ", None), P())
    return jax.shard_map(
        local,
        mesh=mesh,
        in_specs=placed,
        out_specs=(P("occ", "grp"), P("occ", "grp")),
        check_vma=False,
    )
```

```python
import functools
import math

import jax
import jax.numpy as jnp
from jax import lax
from jax.experimental import pallas as pl
from jax.experimental.pallas import tpu as pltpu
from jax.sharding import PartitionSpec as P

MESH = pl.DeviceIdType.MESH


def shifted(x, axis, by):
    size = lax.axis_size(axis)
    return lax.ppermute(x, axis, [(i, (i + by) % size) for i in range(size)])


def block_plan(n_vir, n_aux, n_cycle, n_group):
    aux_local, vir_local = n_aux // n_cycle, n_vir // n_group
    joined = 128 // math.gcd(aux_local, 128)
    lanes = joined * aux_local // 128
    halves = 2 if vir_local % (32 * joined) == 0 else 1
    return aux_local, vir_local, joined, lanes, halves, vir_local // joined // halves


def pair_kernel(
    n_cycle, n_group, chunks,
    own_ref, rot_ref, energy_ref, start_ref, vir_row_ref, dens_out, blocks_out,
    near, far, total, stage, vir_col_ref, near_ss, near_rs, far_ss, far_rs,
):
    cyc = lax.axis_index("occ")
    grp = lax.axis_index("grp")
    odd = lax.rem(cyc, 2)
    mate = cyc + 1 - 2 * odd
    ahead = lax.rem(cyc + 2, n_cycle)
    behind = lax.rem(cyc + n_cycle - 2, n_cycle)
    size = own_ref.shape[0] // chunks
    barrier = pltpu.get_barrier_semaphore()
    for other in (mate, ahead, behind):
        pl.semaphore_signal(barrier, inc=1, device_id=(other, grp), device_id_type=MESH)
    pl.semaphore_wait(barrier, 3)

    def part(c):
        return pl.ds(c * size, size)

    def far_copy(c):
        return pltpu.make_async_remote_copy(
            src_ref=rot_ref.at[part(c)], dst_ref=far.at[part(c)],
            send_sem=far_ss.at[c], recv_sem=far_rs.at[c],
            device_id=(ahead, grp), device_id_type=MESH,
        )

    def near_copy(c, source):
        return pltpu.make_async_remote_copy(
            src_ref=source.at[part(c)], dst_ref=near.at[part(c)],
            send_sem=near_ss.at[c], recv_sem=near_rs.at[c],
            device_id=(mate, grp), device_id_type=MESH,
        )

    for c in range(chunks):
        far_copy(c).start()

        @pl.when(odd == 0)
        def _():
            near_copy(c, rot_ref).start()

    n_vir, n_aux = own_ref.shape
    vir_col_ref[...] = jnp.broadcast_to(vir_row_ref[...], (128, n_vir)).T
    shift = lax.rem(start_ref[0], n_cycle)
    own_energy = energy_ref[cyc * n_group + grp]
    tall = min(256, n_vir)
    across = (((1,), (1,)), ((), ()))

    def term(other, step_no, put):
        place = lax.rem(cyc - shift - step_no + 2 * n_cycle, n_cycle)
        energy = own_energy + energy_ref[place * n_group + grp]

        @pl.loop(0, n_vir // tall)
        def _(k):
            at = pl.ds(pl.multiple_of(k * tall, tall), tall)
            straight = lax.dot_general(
                own_ref[at, :], other[...], across, preferred_element_type=jnp.float32
            )
            crossed = lax.dot_general(
                other[at, :], own_ref[...], across, preferred_element_type=jnp.float32
            )
            denominator = energy - vir_col_ref[at, 0:1] - vir_row_ref[...]
            combined = ((2.0 * straight - crossed) / denominator).astype(jnp.bfloat16)
            put(at, jnp.dot(combined, other[...], preferred_element_type=jnp.float32))

    def put_first(at, value):
        total[at, :] = value

    def put_next(at, value):
        total[at, :] += value

    def put_last(at, value):
        value = total[at, :] + value
        for b in range(n_aux // 128):
            stage[pl.ds(b * n_vir + at.start, tall), :] = value[:, b * 128:(b + 1) * 128]
        dens_out[at, :] = value.astype(dens_out.dtype)

    term(rot_ref, 0, put_first)
    for c in range(chunks):
        far_copy(c).wait_recv()

        @pl.when(odd == 1)
        def _():
            near_copy(c, far).start()

    term(far, 2, put_next)
    for c in range(chunks):
        near_copy(c, rot_ref).wait_recv()
    term(near, 1, put_last)

    aux_local, vir_local, joined, lanes, halves, tall_block = block_plan(
        n_vir, n_aux, n_cycle, n_group
    )

    @pl.loop(0, n_group * halves)
    def _(k):
        g, h = k // halves, lax.rem(k, halves)
        first = k * (tall_block * joined)
        picked = [
            jnp.concatenate(
                [
                    stage[pl.ds(b * n_vir + first + j, tall_block, stride=joined), :]
                    for b in range(n_aux // 128)
                ],
                axis=1,
            )
            for j in range(joined)
        ]
        for o in range(n_cycle):
            wide = jnp.concatenate(
                [piece[:, o * aux_local:(o + 1) * aux_local] for piece in picked], axis=1
            ).astype(blocks_out.dtype)
            for c in range(lanes):
                blocks_out[o * n_group + g, h * lanes + c] = wide[:, c * 128:(c + 1) * 128]

    for c in range(chunks):
        far_copy(c).wait_send()
        near_copy(c, rot_ref).wait_send()


def pair_densities(n_cycle, n_group, own_rows, rotated, occ_energy, vir_energy, window_start):
    n_vir, n_aux = own_rows.shape
    chunks = 8
    _, _, _, lanes, halves, tall_block = block_plan(n_vir, n_aux, n_cycle, n_group)
    smem = pl.BlockSpec(memory_space=pltpu.SMEM)
    vmem = pl.BlockSpec(memory_space=pltpu.VMEM)
    dma = pltpu.SemaphoreType.DMA
    block = pltpu.VMEM((n_vir, n_aux), jnp.bfloat16)
    return pl.pallas_call(
        functools.partial(pair_kernel, n_cycle, n_group, chunks),
        out_shape=(
            jax.ShapeDtypeStruct((n_vir, n_aux), jnp.bfloat16),
            jax.ShapeDtypeStruct(
                (n_cycle * n_group, halves * lanes, tall_block, 128), jnp.bfloat16
            ),
        ),
        in_specs=[vmem, vmem, smem, smem, vmem],
        out_specs=(vmem, vmem),
        scratch_shapes=[
            block, block, pltpu.VMEM((n_vir, n_aux), jnp.float32),
            pltpu.VMEM((n_aux // 128 * n_vir, 128), jnp.float32),
            pltpu.VMEM((n_vir, 128), jnp.float32),
            dma((chunks,)), dma((chunks,)), dma((chunks,)), dma((chunks,)),
        ],
        compiler_params=pltpu.CompilerParams(
            collective_id=0, has_side_effects=True, vmem_limit_bytes=24 * 1024 * 1024
        ),
    )(own_rows, rotated, occ_energy, window_start, vir_energy[None, :])


def exchange_kernel(
    n_cycle, n_group, inner, halves, lanes, step_rows,
    blocks_ref, dens_hbm, own_ref, int_ref, aux_out, lag_out,
    dens_ref, own_block, load_sem, dens_recv, dens_f32, pair_send, pair_recv, aux_sum, plane_send, plane_recv, plane_sum,
    line_send, line_recv, int_vmem, lag_acc, lag_send, lag_recv,
    int_sem, dens_ss, dens_rs, pair_ss, pair_rs, plane_ss, plane_rs, line_ss, line_rs,
    lag_ss, lag_rs,
):
    cyc = lax.axis_index("occ")
    grp = lax.axis_index("grp")
    n_dev = n_cycle * n_group
    me = cyc * n_group + grp
    outer = n_cycle // inner
    seat = lax.rem(cyc, inner)
    plane = cyc // inner
    tall_block = blocks_ref.shape[2]
    half_rows = lanes * tall_block
    rows = halves * half_rows
    depth = step_rows * lanes * 128
    n_steps = halves * tall_block // step_rows

    def int_copy(k):
        part = pl.ds(pl.multiple_of(k * depth, depth), depth)
        return pltpu.make_async_copy(int_ref.at[part], int_vmem.at[part], int_sem.at[k])

    dens_load = pltpu.make_async_copy(dens_hbm, dens_ref, load_sem.at[0])
    block_load = pltpu.make_async_copy(blocks_ref.at[me], own_block, load_sem.at[1])
    dens_load.start()
    block_load.start()
    barrier = pltpu.get_barrier_semaphore()

    @pl.loop(1, n_dev)
    def _(s):
        d = lax.rem(me + s, n_dev)
        pl.semaphore_signal(
            barrier, inc=1, device_id=(d // n_group, lax.rem(d, n_group)), device_id_type=MESH
        )

    @pl.loop(0, n_steps)
    def _(k):
        int_copy(k).start()

    pl.semaphore_wait(barrier, n_dev - 1)

    def dens_copy(h, s):
        d = lax.rem(me + s, n_dev)
        part = pl.ds(h * lanes, lanes)
        return pltpu.make_async_remote_copy(
            src_ref=blocks_ref.at[d, part], dst_ref=dens_recv.at[s - 1, part],
            send_sem=dens_ss.at[h, s - 1], recv_sem=dens_rs.at[h, s - 1],
            device_id=(d // n_group, lax.rem(d, n_group)), device_id_type=MESH,
        )

    def pair_copy(s):
        return pltpu.make_async_remote_copy(
            src_ref=pair_send.at[s - 1], dst_ref=pair_recv.at[s - 1],
            send_sem=pair_ss.at[s - 1], recv_sem=pair_rs.at[s - 1],
            device_id=(cyc, lax.rem(grp + s, n_group)), device_id_type=MESH,
        )

    def plane_copy(s):
        q = lax.rem(seat + s, inner)
        return pltpu.make_async_remote_copy(
            src_ref=plane_send.at[s - 1], dst_ref=plane_recv.at[s - 1],
            send_sem=plane_ss.at[s - 1], recv_sem=plane_rs.at[s - 1],
            device_id=(plane * inner + q, grp), device_id_type=MESH,
        )

    def line_copy(s):
        z = lax.rem(plane + s, outer)
        return pltpu.make_async_remote_copy(
            src_ref=line_send.at[s - 1], dst_ref=line_recv.at[s - 1],
            send_sem=line_ss.at[s - 1], recv_sem=line_rs.at[s - 1],
            device_id=(z * inner + seat, grp), device_id_type=MESH,
        )

    def lag_copy(s):
        d = lax.rem(me + s, n_dev)
        return pltpu.make_async_remote_copy(
            src_ref=lag_send.at[d], dst_ref=lag_recv.at[s - 1],
            send_sem=lag_ss.at[s - 1], recv_sem=lag_rs.at[s - 1],
            device_id=(d // n_group, lax.rem(d, n_group)), device_id_type=MESH,
        )

    for h in range(halves):
        @pl.loop(1, n_dev)
        def _(s):
            dens_copy(h, s).start()

    def own_part(g):
        width = aux_out.shape[1]
        if len(own_ref.shape) == 3:
            return own_ref[g]
        return own_ref[:, pl.ds(pl.multiple_of(g * width, 128), width)]

    def aux_columns(g):
        return lax.dot_general(
            dens_ref[...], own_part(g), (((0,), (0,)), ((), ())),
            preferred_element_type=jnp.float32,
        ).reshape(aux_sum.shape)

    dens_load.wait()
    block_load.wait()
    for s in range(1, n_group):
        pair_send[s - 1] = aux_columns(lax.rem(grp + s, n_group))
        pair_copy(s).start()
    aux_sum[...] = aux_columns(grp)
    for s in range(1, n_group):
        pair_copy(s).wait_recv()

        @pl.loop(0, n_cycle)
        def _(o):
            aux_sum[o] += pair_recv[s - 1, o]

    for s in range(1, inner):
        q = lax.rem(seat + s, inner)

        @pl.loop(0, outer)
        def _(z):
            plane_send[s - 1, z] = aux_sum[z * inner + q].astype(plane_send.dtype)

        plane_copy(s).start()

    def take_half(h):
        part = pl.ds(h * lanes, lanes)
        own_at = pl.ds(me * rows + h * half_rows, half_rows)
        dens_f32[own_at, :] = own_block[part].astype(jnp.float32).reshape(half_rows, 128)

        @pl.loop(1, n_dev)
        def _(s):
            dens_copy(h, s).wait_recv()
            source = lax.rem(me - s + n_dev, n_dev)
            at = pl.ds(source * rows + h * half_rows, half_rows)
            block = dens_recv[s - 1, part].astype(jnp.float32)
            dens_f32[at, :] = block.reshape(half_rows, 128)

        steps = n_steps // halves

        @pl.loop(h * steps, (h + 1) * steps)
        def _(k):
            int_copy(k).wait()
            pieces = [
                dens_f32[
                    pl.ds(
                        h * half_rows + c * tall_block + (k - h * steps) * step_rows + j,
                        n_dev, stride=rows,
                    ), :
                ]
                for j in range(step_rows) for c in range(lanes)
            ]
            left = jnp.concatenate(pieces, axis=1).astype(jnp.bfloat16)
            at = pl.ds(pl.multiple_of(k * depth, depth), depth)
            lag_acc[...] += jnp.dot(left, int_vmem[at, :], preferred_element_type=jnp.float32)

    lag_acc[...] = jnp.zeros_like(lag_acc)
    for h in range(halves - 1):
        take_half(h)

    for s in range(1, inner):
        plane_copy(s).wait_recv()

    @pl.loop(0, outer)
    def _(z):
        block = aux_sum[z * inner + seat]
        for s in range(1, inner):
            block = block + plane_recv[s - 1, z].astype(jnp.float32)
        plane_sum[z] = block

    for s in range(1, outer):
        line_send[s - 1] = plane_sum[lax.rem(plane + s, outer)].astype(line_send.dtype)
        line_copy(s).start()

    take_half(halves - 1)

    orb_block = lag_out.shape[1]
    for o in range(n_cycle):
        for g in range(n_group):
            lag_send[o * n_group + g] = lag_acc[
                o * n_group:(o + 1) * n_group, g * orb_block:(g + 1) * orb_block
            ]

    @pl.loop(1, n_dev)
    def _(s):
        lag_copy(s).start()

    aux_total = plane_sum[plane]
    for s in range(1, outer):
        line_copy(s).wait_recv()
        aux_total = aux_total + line_recv[s - 1].astype(jnp.float32)
    aux_out[...] = aux_total

    lag_out[...] = lag_send[me]

    @pl.loop(1, n_dev)
    def _(s):
        lag_copy(s).wait_recv()
        lag_out[...] += lag_recv[s - 1]

    for s in range(1, n_group):
        pair_copy(s).wait_send()
    for s in range(1, inner):
        plane_copy(s).wait_send()
    for s in range(1, outer):
        line_copy(s).wait_send()

    @pl.loop(1, n_dev)
    def _(s):
        for h in range(halves):
            dens_copy(h, s).wait_send()
        lag_copy(s).wait_send()


def exchange(n_cycle, n_group, dens_blocks, density, own_columns, int_rows):
    n_dev = dens_blocks.shape[0]
    n_vir, n_aux = density.shape
    row_block = n_aux // n_cycle
    col_block = n_aux // n_group
    depth, n_orb = int_rows.shape
    orb_block = n_orb // n_group
    _, _, _, lanes, halves, tall_block = block_plan(n_vir, n_aux, n_cycle, n_group)
    step_rows = 2 if tall_block % 2 == 0 else 1
    rows = halves * lanes * tall_block
    inner = 4 if n_cycle % 4 == 0 else 1
    outer = n_cycle // inner
    tile = (row_block, col_block)
    anywhere = pl.BlockSpec(memory_space=pl.ANY)
    vmem = pl.BlockSpec(memory_space=pltpu.VMEM)
    dma = pltpu.SemaphoreType.DMA
    return pl.pallas_call(
        functools.partial(
            exchange_kernel, n_cycle, n_group, inner, halves, lanes, step_rows
        ),
        out_shape=(
            jax.ShapeDtypeStruct(tile, jnp.float32),
            jax.ShapeDtypeStruct((n_group, orb_block), jnp.float32),
        ),
        in_specs=[anywhere, anywhere, vmem, anywhere],
        out_specs=(vmem, vmem),
        scratch_shapes=[
            pltpu.VMEM((n_vir, n_aux), jnp.bfloat16),
            pltpu.VMEM(dens_blocks.shape[1:], jnp.bfloat16),
            dma((2,)),
            pltpu.VMEM((n_dev - 1,) + dens_blocks.shape[1:], jnp.bfloat16),
            pltpu.VMEM((n_dev * rows, 128), jnp.float32),
            pltpu.VMEM((n_group - 1, n_cycle) + tile, jnp.float32),
            pltpu.VMEM((n_group - 1, n_cycle) + tile, jnp.float32),
            pltpu.VMEM((n_cycle,) + tile, jnp.float32),
            pltpu.VMEM((inner - 1, outer) + tile, jnp.bfloat16),
            pltpu.VMEM((inner - 1, outer) + tile, jnp.bfloat16),
            pltpu.VMEM((outer,) + tile, jnp.float32),
            pltpu.VMEM((outer - 1,) + tile, jnp.bfloat16),
            pltpu.VMEM((outer - 1,) + tile, jnp.bfloat16),
            pltpu.VMEM((depth, n_orb), jnp.bfloat16),
            pltpu.VMEM((n_dev, n_orb), jnp.float32),
            pltpu.VMEM((n_dev, n_group, orb_block), jnp.float32),
            pltpu.VMEM((n_dev - 1, n_group, orb_block), jnp.float32),
            dma((halves * tall_block // step_rows,)),
            dma((halves, n_dev - 1)), dma((halves, n_dev - 1)),
            dma((n_group - 1,)), dma((n_group - 1,)),
            dma((inner - 1,)), dma((inner - 1,)),
            dma((outer - 1,)), dma((outer - 1,)),
            dma((n_dev - 1,)), dma((n_dev - 1,)),
        ],
        compiler_params=pltpu.CompilerParams(
            collective_id=1, has_side_effects=True, vmem_limit_bytes=42 * 1024 * 1024
        ),
    )(dens_blocks, density, own_columns, int_rows)


def local(b_factors, occ_energy, vir_energy, integrals, window_start):
    n_cycle = lax.axis_size("occ")
    n_group = lax.axis_size("grp")
    offset = jnp.mod(window_start[0], n_cycle)
    own_rows = b_factors[0]
    n_vir, n_aux = own_rows.shape
    rotated = lax.switch(
        offset,
        [(lambda x: x)]
        + [functools.partial(lambda by, x: shifted(x, "occ", by), by) for by in range(1, n_cycle)],
        own_rows,
    )
    density, dens_blocks = pair_densities(
        n_cycle, n_group, own_rows, rotated, occ_energy, vir_energy, window_start
    )
    col_block = n_aux // n_group
    own_columns = own_rows
    if col_block % 128:
        own_columns = own_rows.reshape(n_vir, n_group, col_block).transpose(1, 0, 2)
    int_rows = integrals.reshape(-1, integrals.shape[2])
    return exchange(n_cycle, n_group, dens_blocks, density, own_columns, int_rows)


def solution(mesh):
    placed = (P(("occ", "grp"), None, None), P(), P(), P("grp", "occ", None), P())
    return jax.shard_map(
        local,
        mesh=mesh,
        in_specs=placed,
        out_specs=(P("occ", "grp"), P("occ", "grp")),
        check_vma=False,
    )
```
